32 devices in a mesh: group: 2 (over x), sec: 16 (over z, y, core).
Axes of the slice: x: 2, y: 2, z: 4, core: 2. Of those that a mesh axis runs over, the one named last changes fastest.
Arguments:
- residual: bfloat16 [4096, 256], P('sec', 'group'), parts along dimension 1, may hold values from -80 to 80
- queries: bfloat16 [256, 4096], P(('group', 'sec')), parts along dimension 0, may hold values from -200 to 200
- new_keys: bfloat16 [256, 512], P(('group', 'sec')), parts along dimension 0, may hold values from -7 to 7
- new_values: bfloat16 [256, 512], P(('group', 'sec')), parts along dimension 0, may hold values from -6 to 6
- cache_keys: bfloat16 [256, 128, 512], P(('group', 'sec')), parts along dimension 0, may hold values from -6 to 6
- cache_values: bfloat16 [256, 128, 512], P(('group', 'sec')), parts along dimension 0, may hold values from -6 to 6
- cache_lengths: int32 [256], P(('group', 'sec')), parts along dimension 0, may hold values from 1 to 128, 4096 in all
- slot_of_row: int32 [256], P('group'), parts along dimension 0, may hold values from 0 to 127, each once
- out_weight: bfloat16 [4096, 4096], P('sec'), may hold values from -0.09375 to 0.09375
- norm_gain: float32 [4096], replicated, may hold values from 0.1 to 1.9
- gate_weight: bfloat16 [28672, 4096], P('sec'), may hold values from -0.09375 to 0.09375
- up_weight: bfloat16 [28672, 4096], P('sec'), may hold values from -0.09375 to 0.09375
- down_weight: bfloat16 [28672, 4096], P('sec'), may hold values from -0.046875 to 0.046875
Outputs:
- layer_out: bfloat16 [4096, 256], P('sec', 'group'), parts along dimension 1
The draws below stay inside these ranges and needn't reach their ends.
There are 2 independent parts, one for each index of `group`. The reference program is written for one: setup_inputs(seed, part) draws one part's arguments, and reference() takes and returns one part's arrays. A program takes and returns all parts, laid end to end along the dimension named above; an argument that names none is the same for every part. Nothing has to cross between parts.
Inputs may be any that keep to these rules, and one draw needn't show every extreme that they name: `slot_of_row`: each of 0 to 127 once. `cache_lengths`: the lengths sum to 4096 and the largest is exactly 128.
All inputs are finite; a program needn't handle non-finite values. No bound on the sum of `cache_lengths` on one device may be relied on, other than what follows from the above.
Results may differ from the reference program's by a relative error of at most 0.0095.
Values may be sent and summed in bfloat16 or wider, within the bound.
No kernel may reach another device: no remote copies, remote signals or barrier semaphores. Data moves between devices by JAX's collectives and lax.ppermute only.
A program may use at most 128 MiB of HBM per device.

```python
import math
import jax
import jax.numpy as jnp
import numpy as np
from jax import lax

D = 4096
H = 32
KVH = 4
HD = 128
FF = 28672
CTX = 128
ROWS = 128


def drawn_parts(key):
    first_keys = jax.random.truncated_normal(jax.random.fold_in(key, 101), -6.0, 6.0, (ROWS, KVH * HD), jnp.float32)
    return first_keys


def draw_cache_keys(key, part):
    first_keys = drawn_parts(key)
    others = jax.random.truncated_normal(jax.random.fold_in(key, 102), -6.0, 6.0, (ROWS, CTX - 1, KVH * HD), jnp.float32)
    return jnp.concatenate([first_keys[:, None, :], others], axis=1).astype(jnp.bfloat16)


def draw_new_keys(key, part):
    drawn = jax.random.truncated_normal(jax.random.fold_in(key, 103), -6.0, 6.0, (ROWS, KVH * HD), jnp.float32)
    return drawn.astype(jnp.bfloat16)


def draw_queries(key, part):
    drawn = jax.random.truncated_normal(jax.random.fold_in(key, 104), -6.0, 6.0, (ROWS, H * HD), jnp.float32)
    return drawn.astype(jnp.bfloat16)


def draw_residual(key, part):
    feature_scale = jnp.exp(jax.random.uniform(jax.random.fold_in(key, 201), (D,), jnp.float32, math.log(0.3), math.log(3.0)))
    row_scale = jnp.exp(jax.random.uniform(jax.random.fold_in(key, 202), (ROWS,), jnp.float32, math.log(0.3), math.log(3.0)))
    values_drawn = jax.random.truncated_normal(jax.random.fold_in(key, 203), -5.0, 5.0, (D, ROWS), jnp.float32)
    rising = 1.0 + 0.75 * jnp.arange(D).astype(jnp.float32) / D
    return (values_drawn * (feature_scale * rising)[:, None] * row_scale[None, :]).astype(jnp.bfloat16)


def raised(entries, key, source, target, parts, factor):
    owner, partner = [(jnp.arange(entries.shape[dim]) // (entries.shape[dim] // parts)).reshape([-1 if axis == dim else 1 for axis in range(entries.ndim)]) for dim in (source, target)]
    chosen = jax.random.permutation(key, parts)[partner]
    strong = (owner == chosen) | (owner == (partner + parts // 2) % parts)
    return jnp.where(strong, factor * entries, entries)


def shard_levels(stream_key, dims, pieces, smallest, high):
    def one(position, parts):
        heights = jax.random.uniform(jax.random.fold_in(jax.random.fold_in(stream_key, 6), position), (parts,), jnp.float32, smallest / len(pieces), high / len(pieces))
        return jnp.repeat(jnp.exp(heights), dims[position] // parts).reshape((-1,) + (1,) * (len(dims) - position - 1))

    gain = one(*pieces[0])
    for cut in pieces[1:]:
        gain = gain * one(*cut)
    return gain


def split_up(number_of, total, reach, slope):
    portions = [(1 << 20) // math.isqrt(standing ** slope) + 1 for standing in range(2, number_of + 1)]
    surplus, counts = total - reach - (number_of - 1), [1] * (number_of - 1)
    while surplus > 0:
        movable = [i for i in range(number_of - 1) if counts[i] < reach]
        mass, remaining = sum([portions[i] for i in movable]), surplus
        for i in movable:
            addition = min(reach - counts[i], max(1, remaining * portions[i] // mass), surplus)
            counts[i] = counts[i] + addition
            surplus = surplus - addition
    return np.array([reach] + counts)


def uneven(rng, amount, total, limit, slope):
    if amount == 2:
        one = jax.random.randint(rng, (), max(1, total - limit), min(limit, total - 1) + 1)
        return jnp.stack([one, total - one])
    tallies = jnp.asarray(split_up(amount, total, limit, slope), jnp.int32)
    twos = (amount - 1) // 2
    giver, receiver = tallies[1:1 + 2 * twos:2], tallies[2:2 + 2 * twos:2]
    margin = jnp.minimum(giver - 1, limit - receiver)
    moved = jax.random.randint(jax.random.fold_in(rng, 1), (twos,), 0, 1 << 20) % (margin + 1)
    tallies = tallies.at[1:1 + 2 * twos:2].set(giver - moved).at[2:2 + 2 * twos:2].set(receiver + moved)
    return tallies[jax.random.permutation(jax.random.fold_in(rng, 2), amount)]


def bell_draw(stream_key, extent, deviation, reach, shards=(), kind=jnp.bfloat16):
    factor_of = shard_levels(stream_key, extent, shards, -0.22, 0.18) if shards else 1.0
    entries = jax.random.normal(stream_key, extent, jnp.float32) * deviation * factor_of
    return jnp.minimum(jnp.maximum(entries, -reach), reach).astype(kind)


def bell_draw_with(rng, dims, deviation, most, split, heavy, held_as=jnp.bfloat16):
    values = deviation * jax.random.normal(rng, dims, jnp.float32)
    if split:
        values = values * shard_levels(rng, dims, split, -0.22, 0.18)
    return jnp.clip(raised(values, jax.random.fold_in(rng, 3), *heavy), -most, most).astype(held_as)


def setup_inputs(seed: int = 0, part: int = 0) -> dict:
    keys = jax.random.split(jax.random.key(seed), 14)
    part_keys = jax.random.split(jax.random.fold_in(keys[13], part), 14)
    return {
        "residual": draw_residual(jax.random.fold_in(jax.random.fold_in(keys[13], part), 71), part),
        "queries": draw_queries(jax.random.fold_in(jax.random.fold_in(keys[13], part), 71), part),
        "new_keys": draw_new_keys(jax.random.fold_in(jax.random.fold_in(keys[13], part), 71), part),
        "new_values": bell_draw(part_keys[3], (ROWS, KVH * HD), 1.0, 6.0, ((0, 16),)),
        "cache_keys": draw_cache_keys(jax.random.fold_in(jax.random.fold_in(keys[13], part), 71), part),
        "cache_values": bell_draw(part_keys[5], (ROWS, CTX, KVH * HD), 1.0, 6.0, ((0, 16),)),
        "cache_lengths": uneven(part_keys[6], ROWS, ROWS * CTX // 4, CTX, 2).astype(jnp.int32),
        "slot_of_row": jax.random.permutation(part_keys[7], ROWS).astype(jnp.int32),
        "out_weight": bell_draw(keys[8], (D, H * HD), (H * HD) ** -0.5, 0.09375, ((0, 16),)),
        "norm_gain": jnp.clip(1.0 + 0.18 * jax.random.normal(keys[9], (D,), jnp.float32), 0.1, 1.9),
        "gate_weight": bell_draw(keys[10], (FF, D), D ** -0.5, 0.09375, ((0, 16),)),
        "up_weight": bell_draw(keys[11], (FF, D), D ** -0.5, 0.09375, ((0, 16),)),
        "down_weight": bell_draw_with(keys[12], (FF, D), FF ** -0.5, 0.046875, ((0, 16),), (0, 1, 16, 2.0)),
    }


EPSILON = 1e-05

def attend(queries, new_keys, new_values, cache_keys, cache_values, cache_lengths):
    row_count = queries.shape[0]
    positions_total = cache_keys.shape[1]
    grouped = H // KVH
    scaling = 1.0 / math.sqrt(HD)
    query_heads = queries.astype(jnp.float32).reshape(row_count, KVH, grouped, HD)
    cached_keys = cache_keys.astype(jnp.float32).reshape(row_count, positions_total, KVH, HD)
    cached_values = cache_values.astype(jnp.float32).reshape(row_count, positions_total, KVH, HD)
    fresh_keys = new_keys.astype(jnp.float32).reshape(row_count, KVH, HD)
    scores = jnp.einsum('rkgd,rpkd->rkgp', query_heads, cached_keys) * scaling
    fresh_score = jnp.einsum('rkgd,rkd->rkg', query_heads, fresh_keys) * scaling
    positions = lax.broadcasted_iota(jnp.int32, scores.shape, 3)
    usable = positions < cache_lengths.astype(jnp.int32)[:, None, None, None]
    highest = jnp.maximum(lax.optimization_barrier(jnp.max(jnp.where(usable, scores, -jnp.inf), axis=3)), fresh_score)
    weights = jnp.where(usable, jnp.exp(scores - highest[..., None]), 0.0)
    fresh_weight = jnp.exp(fresh_score - highest)
    summed = lax.optimization_barrier(jnp.sum(weights, axis=3)) + fresh_weight
    weights = (weights / summed[..., None]).astype(jnp.bfloat16)
    fresh_weight = (fresh_weight / summed).astype(jnp.bfloat16)
    mixture = jnp.einsum('rkgp,rpkd->rkgd', weights.astype(jnp.float32), cached_values)
    mixture = mixture + fresh_weight.astype(jnp.float32)[..., None] * new_values.astype(jnp.float32).reshape(row_count, KVH, 1, HD)
    return mixture.reshape(row_count, H * HD).astype(jnp.bfloat16)

def reference(residual, queries, new_keys, new_values, cache_keys, cache_values, cache_lengths, slot_of_row, out_weight, norm_gain, gate_weight, up_weight, down_weight):
    attended = attend(queries, new_keys, new_values, cache_keys, cache_values, cache_lengths)
    ordered = jnp.take(attended, slot_of_row.astype(jnp.int32), axis=0)
    branch = lax.dot_general(out_weight, ordered, (((1,), (1,)), ((), ())), preferred_element_type=jnp.float32)
    stream = (residual.astype(jnp.float32) + branch).astype(jnp.bfloat16)
    widened = stream.astype(jnp.float32)
    mean_square = lax.optimization_barrier(jnp.mean(widened * widened, axis=0))
    normed = (widened * lax.rsqrt(mean_square + EPSILON)[None, :] * norm_gain[:, None]).astype(jnp.bfloat16)
    gate_sum = jnp.dot(gate_weight, normed, preferred_element_type=jnp.float32)
    up_sum = jnp.dot(up_weight, normed, preferred_element_type=jnp.float32)
    hidden = (jax.nn.silu(gate_sum) * up_sum).astype(jnp.bfloat16)
    lowered = lax.dot_general(down_weight, hidden, (((0,), (0,)), ((), ())), preferred_element_type=jnp.float32)
    return (widened + lowered).astype(jnp.bfloat16)
```

```python
import math

import jax
import jax.numpy as jnp
from jax import lax
from jax.sharding import PartitionSpec as P

H = 32
KVH = 4
HD = 128


EPSILON = 1e-05


def attend(queries, new_keys, new_values, cache_keys, cache_values, cache_lengths):
    row_count = queries.shape[0]
    positions_total = cache_keys.shape[1]
    grouped = H // KVH
    scaling = 1.0 / math.sqrt(HD)
    query_heads = queries.reshape(row_count, KVH, grouped, HD)
    cached_keys = cache_keys.reshape(row_count, positions_total, KVH, HD)
    cached_values = cache_values.reshape(row_count, positions_total, KVH, HD)
    fresh_keys = new_keys.reshape(row_count, KVH, HD)
    scores = (
        jnp.einsum("rkgd,rpkd->rkgp", query_heads, cached_keys, preferred_element_type=jnp.float32)
        * scaling
    )
    fresh_score = (
        jnp.einsum("rkgd,rkd->rkg", query_heads, fresh_keys, preferred_element_type=jnp.float32)
        * scaling
    )
    positions = lax.broadcasted_iota(jnp.int32, scores.shape, 3)
    usable = positions < cache_lengths[:, None, None, None]
    highest = jnp.maximum(jnp.max(jnp.where(usable, scores, -jnp.inf), axis=3), fresh_score)
    weights = jnp.where(usable, jnp.exp(scores - highest[..., None]), 0.0)
    fresh_weight = jnp.exp(fresh_score - highest)
    summed = jnp.sum(weights, axis=3) + fresh_weight
    weights = (weights / summed[..., None]).astype(jnp.bfloat16)
    fresh_weight = (fresh_weight / summed).astype(jnp.bfloat16)
    mixture = jnp.einsum(
        "rkgp,rpkd->rkgd", weights, cached_values, preferred_element_type=jnp.float32
    )
    mixture = mixture + fresh_weight.astype(jnp.float32)[..., None] * new_values.astype(
        jnp.float32
    ).reshape(row_count, KVH, 1, HD)
    return mixture.reshape(row_count, H * HD).astype(jnp.bfloat16)


class Chips:
    def __init__(self, devices):
        self.devices = devices
        self.count = devices // 2
        assert devices == 2 * self.count and self.count & (self.count - 1) == 0
        far = list(range(self.count - 1, 1, -1))
        self.steps = list(zip(far[0::2], far[1::2]))
        self.core_swap = [(i, i ^ 1) for i in range(devices)]
        self.near = [(i, i ^ 2) for i in range(devices)] if self.count > 1 else None

    def pairs(self, step):
        return [(i, i ^ (2 * step[i % 2])) for i in range(self.devices)]

    def swap(self, x):
        return lax.ppermute(x, "sec", self.core_swap)


def gather_blocks(chips, x):
    me = lax.axis_index("sec")
    core = me % 2
    chip = me // 2
    m = x.shape[0]
    other = chips.swap(x)
    both = jnp.where(core == 0, jnp.concatenate([x, other]), jnp.concatenate([other, x]))
    received = [lax.ppermute(both, "sec", chips.pairs(s)) for s in chips.steps]
    result = jnp.zeros((chips.count, 2 * m) + x.shape[1:], x.dtype)
    put = lambda r, v, at: lax.dynamic_update_slice(r, v[None], (at,) + (0,) * v.ndim)
    result = put(result, both, chip)
    if chips.count > 1:
        half = jnp.where(core == 0, both[:m], both[m:])
        near = lax.ppermute(half, "sec", chips.near)
    swapped = [chips.swap(r) for r in received]
    for s, r, w in zip(chips.steps, received, swapped):
        result = put(result, r, chip ^ jnp.where(core == 0, s[0], s[1]))
        result = put(result, w, chip ^ jnp.where(core == 0, s[1], s[0]))
    if chips.count > 1:
        far = chips.swap(near)
        near = jnp.where(core == 0, jnp.concatenate([near, far]), jnp.concatenate([far, near]))
        result = put(result, near, chip ^ 1)
    return result.reshape((chips.count * 2 * m,) + x.shape[1:])


def scatter_sums(chips, partial):
    me = lax.axis_index("sec")
    core = me % 2
    chip = me // 2
    blocks = partial.reshape((chips.count, -1) + partial.shape[1:])
    m = blocks.shape[1] // 2
    take = lambda at: lax.dynamic_index_in_dim(blocks, at, 0, keepdims=False)
    total = None
    for s in chips.steps:
        mine = take(chip ^ jnp.where(core == 0, s[0], s[1]))
        theirs = take(chip ^ jnp.where(core == 0, s[1], s[0])).astype(jnp.bfloat16)
        summed = (mine + chips.swap(theirs).astype(jnp.float32)).astype(jnp.bfloat16)
        got = lax.ppermute(summed, "sec", chips.pairs(s)).astype(jnp.float32)
        total = got if total is None else total + got
    own = take(chip)
    if chips.count > 1:
        near = take(chip ^ 1)
        mine = jnp.where(core == 0, near[:m], near[m:])
        theirs = jnp.where(core == 0, near[m:], near[:m]).astype(jnp.bfloat16)
        summed = (mine + chips.swap(theirs).astype(jnp.float32)).astype(jnp.bfloat16)
        got = lax.ppermute(summed, "sec", chips.near).astype(jnp.float32)
    else:
        got = 0.0
    if total is not None:
        own = own + total
    mine = jnp.where(core == 0, own[:m], own[m:])
    theirs = jnp.where(core == 0, own[m:], own[:m]).astype(jnp.bfloat16)
    return mine + got + chips.swap(theirs).astype(jnp.float32)


def on_device(
    residual,
    queries,
    new_keys,
    new_values,
    cache_keys,
    cache_values,
    cache_lengths,
    slot_of_row,
    out_weight,
    norm_gain,
    gate_weight,
    up_weight,
    down_weight,
):
    chips = Chips(lax.axis_size("sec"))
    attended = attend(queries, new_keys, new_values, cache_keys, cache_values, cache_lengths)
    gathered_slots = gather_blocks(chips, attended)
    slots = gathered_slots.shape[0]
    pick = (slot_of_row[:, None] == lax.broadcasted_iota(jnp.int32, (slots, slots), 1)).astype(
        jnp.bfloat16
    )
    ordered = jnp.dot(pick, gathered_slots, preferred_element_type=jnp.float32).astype(jnp.bfloat16)
    branch = lax.dot_general(
        out_weight, ordered, (((1,), (1,)), ((), ())), preferred_element_type=jnp.float32
    )
    stream = (residual.astype(jnp.float32) + branch).astype(jnp.bfloat16)
    gathered = gather_blocks(chips, stream)
    widened_all = gathered.astype(jnp.float32)
    mean_square = jnp.mean(widened_all * widened_all, axis=0)
    normed_all = (
        widened_all * lax.rsqrt(mean_square + EPSILON)[None, :] * norm_gain[:, None]
    ).astype(jnp.bfloat16)
    gate_sum = jnp.dot(gate_weight, normed_all, preferred_element_type=jnp.float32)
    up_sum = jnp.dot(up_weight, normed_all, preferred_element_type=jnp.float32)
    hidden = (jax.nn.silu(gate_sum) * up_sum).astype(jnp.bfloat16)
    lowered = scatter_sums(
        chips,
        lax.dot_general(
            down_weight, hidden, (((0,), (0,)), ((), ())), preferred_element_type=jnp.float32
        ),
    )
    return (stream.astype(jnp.float32) + lowered).astype(jnp.bfloat16)


def solution(mesh):
    in_specs = (
        P("sec", "group"),
        P(("group", "sec"), None),
        P(("group", "sec"), None),
        P(("group", "sec"), None),
        P(("group", "sec"), None, None),
        P(("group", "sec"), None, None),
        P(("group", "sec")),
        P("group"),
        P("sec", None),
        P(),
        P("sec", None),
        P("sec", None),
        P("sec", None),
    )
    out_specs = P("sec", "group")
    return jax.shard_map(
        on_device, mesh=mesh, in_specs=in_specs, out_specs=out_specs, check_vma=False
    )
```

```python
import functools
import math

import jax
import jax.numpy as jnp
from jax import lax
from jax.experimental import pallas as pl
from jax.experimental.pallas import tpu as pltpu
from jax.sharding import PartitionSpec as P

H = 32
KVH = 4
HD = 128

EPSILON = 1e-05

F32 = jnp.float32
BF16 = jnp.bfloat16
NT = (((1,), (1,)), ((), ()))
MIB = 1 << 20


def params(mib, grid=0):
    return pltpu.CompilerParams(
        vmem_limit_bytes=mib * MIB,
        dimension_semantics=("arbitrary",) * grid if grid else None,
    )


class Chips:
    def __init__(self, devices):
        self.devices = devices
        self.count = devices // 2
        assert devices == 2 * self.count and self.count & (self.count - 1) == 0
        assert self.count > 2
        far = list(range(self.count - 1, 1, -1))
        self.steps = list(zip(far[0::2], far[1::2]))
        self.core_swap = [(i, i ^ 1) for i in range(devices)]
        self.near_pairs = [(i, i ^ 2) for i in range(devices)]
        self.me = lax.axis_index("sec")
        self.core = self.me % 2
        self.chip = self.me // 2

    def swap(self, x):
        return lax.ppermute(x, "sec", self.core_swap)

    def step(self, x, distances):
        pairs = [(i, i ^ (2 * distances[i % 2])) for i in range(self.devices)]
        return lax.ppermute(x, "sec", pairs)

    def near(self, x):
        return lax.ppermute(x, "sec", self.near_pairs)

    def distances(self, mine):
        first = jnp.array([s[0] for s in self.steps], jnp.int32)
        second = jnp.array([s[1] for s in self.steps], jnp.int32)
        return jnp.where((self.core == 0) == mine, first, second)


def attention_kernel(lens_ref, q_ref, nk_ref, nv_ref, k_ref, v_ref, o_ref):
    slots, positions = k_ref.shape[0], k_ref.shape[1]
    grouped = H // KVH
    rows = grouped * slots
    scaling = 1.0 / math.sqrt(HD)
    row_slot = lax.broadcasted_iota(jnp.int32, (rows, positions), 0) % slots
    position = lax.broadcasted_iota(jnp.int32, (rows, positions), 1)
    bias = jnp.concatenate(
        [
            jnp.where((row_slot == s) & (position < lens_ref[s]), 0.0, -jnp.inf)
            for s in range(slots)
        ],
        axis=1,
    )
    for k in range(KVH):
        at = slice(k * HD, (k + 1) * HD)
        heads = [slice((k * grouped + g) * HD, (k * grouped + g + 1) * HD) for g in range(grouped)]
        query = jnp.concatenate([q_ref[:, h].astype(F32) for h in heads], axis=0)
        keys = k_ref[:, :, at].reshape(slots * positions, HD)
        values = v_ref[:, :, at].reshape(slots * positions, HD)
        scores = lax.dot_general(query.astype(BF16), keys, NT, preferred_element_type=F32)
        scores = scores * scaling + bias
        new_key = jnp.concatenate([nk_ref[:, at].astype(F32)] * grouped, axis=0)
        fresh = jnp.sum(query * new_key, axis=1, keepdims=True) * scaling
        highest = jnp.maximum(jnp.max(scores, axis=1, keepdims=True), fresh)
        weights = jnp.exp(scores - highest)
        fresh_weight = jnp.exp(fresh - highest)
        inverse = 1.0 / (jnp.sum(weights, axis=1, keepdims=True) + fresh_weight)
        probs = (weights * inverse).astype(BF16)
        fresh_prob = (fresh_weight * inverse).astype(BF16).astype(F32)
        mixture = jnp.dot(probs, values, preferred_element_type=F32)
        new_value = jnp.concatenate([nv_ref[:, at].astype(F32)] * grouped, axis=0)
        mixture = mixture + fresh_prob * new_value
        for g, h in enumerate(heads):
            o_ref[:, h] = mixture[g * slots : (g + 1) * slots].astype(BF16)


def attend(queries, new_keys, new_values, cache_keys, cache_values, cache_lengths):
    vmem = pl.BlockSpec(memory_space=pltpu.VMEM)
    return pl.pallas_call(
        attention_kernel,
        in_specs=[pl.BlockSpec(memory_space=pltpu.SMEM)] + [vmem] * 5,
        out_specs=vmem,
        out_shape=jax.ShapeDtypeStruct(queries.shape, BF16),
        compiler_params=params(24),
        name="attention",
    )(cache_lengths, queries, new_keys, new_values, cache_keys, cache_values)


def projection_kernel(pieces, pick_ref, weight_ref, residual_ref, *refs):
    piece_refs, o_ref, slots_ref = refs[:pieces], refs[pieces], refs[pieces + 1]
    at = 0
    for i, ref in enumerate(piece_refs):
        if i == pieces - 2:
            both = jnp.concatenate([ref[...].astype(F32), piece_refs[i + 1][...].astype(F32)])
            slots_ref[at : at + both.shape[0], :] = both.astype(BF16)
            break
        slots_ref[at : at + ref.shape[0], :] = ref[...]
        at += ref.shape[0]
    width = weight_ref.shape[1]
    part = min(width, 1024)
    total = residual_ref[...].astype(F32).T
    pick = pick_ref[...]
    for c in range(0, width, part):
        ordered = jnp.dot(pick, slots_ref[:, c : c + part], preferred_element_type=F32)
        total += lax.dot_general(
            ordered.astype(BF16), weight_ref[:, c : c + part], NT, preferred_element_type=F32
        )
    o_ref[...] = total.astype(BF16)


def project(pick, out_weight, residual, pieces):
    vmem = pl.BlockSpec(memory_space=pltpu.VMEM)
    m, rows = residual.shape
    slots = pick.shape[1]
    return pl.pallas_call(
        functools.partial(projection_kernel, len(pieces)),
        in_specs=[vmem] * (3 + len(pieces)),
        out_specs=vmem,
        out_shape=jax.ShapeDtypeStruct((rows, m), BF16),
        scratch_shapes=[pltpu.VMEM((slots, out_weight.shape[1]), BF16)],
        compiler_params=params(24),
        name="projection",
    )(pick, out_weight, residual, *pieces)


def hidden_kernel(blocks, ids_ref, gain_ref, *refs):
    piece_refs = refs[: blocks + 2]
    gate_ref, up_ref, o_ref, x_ref, scale_ref = refs[blocks + 2 :]
    wide = gain_ref.shape[2]

    @pl.when(pl.program_id(0) == 0)
    def _():
        squares = None

        def place(value, at):
            x_ref[:, pl.ds(pl.multiple_of(at * wide, 128), wide)] = (
                value * gain_ref[at]
            ).astype(BF16)
            return value * value

        for i in range(blocks):
            square = place(piece_refs[i][...].astype(F32), ids_ref[i])
            squares = square if squares is None else squares + square
        mine, other = (piece_refs[blocks + i][...].astype(F32) for i in range(2))
        first = ids_ref[blocks + 1] == 0
        near = jnp.concatenate(
            [jnp.where(first, mine, other), jnp.where(first, other, mine)], axis=1
        )
        squares += place(near, ids_ref[blocks])
        mean = jnp.sum(squares, axis=1, keepdims=True) * (1.0 / x_ref.shape[1])
        scale_ref[...] = jnp.broadcast_to(lax.rsqrt(mean + EPSILON), scale_ref.shape)

    scale = scale_ref[:, :1]
    gate = lax.dot_general(x_ref[...], gate_ref[...], NT, preferred_element_type=F32) * scale
    up = lax.dot_general(x_ref[...], up_ref[...], NT, preferred_element_type=F32) * scale
    o_ref[...] = (gate / (1.0 + jnp.exp(-gate)) * up).astype(BF16)


def hidden_units(ids, gain, pieces, gate_weight, up_weight):
    vmem = pl.BlockSpec(memory_space=pltpu.VMEM)
    units, width = gate_weight.shape
    rows = pieces[0].shape[0]
    tile = 256 if units % 256 == 0 else units
    weight = pl.BlockSpec((tile, width), lambda i: (i, 0))
    return pl.pallas_call(
        functools.partial(hidden_kernel, len(pieces) - 2),
        grid=(units // tile,),
        in_specs=[pl.BlockSpec(memory_space=pltpu.SMEM)]
        + [vmem] * (1 + len(pieces))
        + [weight, weight],
        out_specs=pl.BlockSpec((rows, tile), lambda i: (0, i)),
        out_shape=jax.ShapeDtypeStruct((rows, units), BF16),
        scratch_shapes=[pltpu.VMEM((rows, width), BF16), pltpu.VMEM((rows, 128), F32)],
        compiler_params=params(40, 1),
        name="hidden",
    )(ids, gain, *pieces, gate_weight, up_weight)


def theirs_kernel(ids_ref, hidden_ref, weight_ref, o_ref):
    o_ref[0] = jnp.dot(hidden_ref[...], weight_ref[...], preferred_element_type=F32).astype(BF16)


def partial_sums(ids, hidden, down_weight, wide):
    rows, units = hidden.shape
    count = ids.shape[0]
    return pl.pallas_call(
        theirs_kernel,
        grid_spec=pltpu.PrefetchScalarGridSpec(
            num_scalar_prefetch=1,
            grid=(count,),
            in_specs=[
                pl.BlockSpec((rows, units), lambda i, ids: (0, 0)),
                pl.BlockSpec((units, wide), lambda i, ids: (0, ids[i])),
            ],
            out_specs=pl.BlockSpec((1, rows, wide), lambda i, ids: (i, 0, 0)),
        ),
        out_shape=jax.ShapeDtypeStruct((count, rows, wide), BF16),
        compiler_params=params(24, 1),
        name="theirs",
    )(ids, hidden, down_weight)


def mine_kernel(steps, ids_ref, hidden_ref, weight_ref, swapped_ref, near_ref, nears_ref, *o_refs):
    i = pl.program_id(0)
    total = jnp.dot(hidden_ref[...], weight_ref[...], preferred_element_type=F32)
    total = (total + swapped_ref[0].astype(F32)).astype(BF16)
    for j in range(steps):

        @pl.when(i == j)
        def _():
            o_refs[j][...] = total

    @pl.when(i == 0)
    def _():
        near = near_ref[0].astype(F32) + nears_ref[0].astype(F32)
        m = near.shape[1] // 2
        o_refs[steps][...] = jnp.where(ids_ref[steps] == 0, near[:, :m], near[:, m:]).astype(BF16)


def chip_sums(ids, hidden, down_weight, own, swapped):
    rows, units = hidden.shape
    wide = own.shape[2]
    steps = own.shape[0] - 2
    const = lambda *at: (lambda i, ids: at)
    return pl.pallas_call(
        functools.partial(mine_kernel, steps),
        grid_spec=pltpu.PrefetchScalarGridSpec(
            num_scalar_prefetch=1,
            grid=(steps,),
            in_specs=[
                pl.BlockSpec((rows, units), const(0, 0)),
                pl.BlockSpec((units, wide), lambda i, ids: (0, ids[i])),
                pl.BlockSpec((1, rows, wide), lambda i, ids: (i, 0, 0)),
                pl.BlockSpec((1, rows, wide), const(steps, 0, 0)),
                pl.BlockSpec((1, rows, wide), const(steps, 0, 0)),
            ],
            out_specs=[pl.BlockSpec((rows, wide), const(0, 0))] * steps
            + [pl.BlockSpec((rows, wide // 2), const(0, 0))],
        ),
        out_shape=[jax.ShapeDtypeStruct((rows, wide), BF16)] * steps
        + [jax.ShapeDtypeStruct((rows, wide // 2), BF16)],
        compiler_params=params(40, 1),
        name="mine",
    )(ids, hidden, down_weight, swapped, own, swapped)


def half_of(core, value):
    m = value.shape[1] // 2
    return jnp.where(core == 0, value[:, :m], value[:, m:])


def received_sum(refs):
    total = refs[0][...].astype(F32)
    for ref in refs[1:]:
        total += ref[...].astype(F32)
    return total


def handover_kernel(core_ref, *refs):
    refs[-1][...] = half_of(1 - core_ref[0], received_sum(refs[:-1])).astype(BF16)


def handover(core, received):
    vmem = pl.BlockSpec(memory_space=pltpu.VMEM)
    rows, wide = received[0].shape
    return pl.pallas_call(
        handover_kernel,
        in_specs=[pl.BlockSpec(memory_space=pltpu.SMEM)] + [vmem] * len(received),
        out_specs=vmem,
        out_shape=jax.ShapeDtypeStruct((rows, wide // 2), BF16),
        compiler_params=params(24),
        name="handover",
    )(core, *received)


def output_kernel(core_ref, stream_ref, own_ref, owns_ref, near_ref, hand_ref, *refs):
    core = core_ref[0]
    total = received_sum(refs[:-1])
    total += own_ref[0].astype(F32) + owns_ref[0].astype(F32)
    total = half_of(core, total) + near_ref[...].astype(F32) + hand_ref[...].astype(F32)
    refs[-1][...] = (stream_ref[...].astype(F32) + total).T.astype(BF16)


def output(core, stream, own, swapped, near, hand, received):
    vmem = pl.BlockSpec(memory_space=pltpu.VMEM)
    rows, m = stream.shape
    last = pl.BlockSpec((1, rows, 2 * m), lambda i: (own.shape[0] - 1, 0, 0))
    return pl.pallas_call(
        output_kernel,
        grid=(1,),
        in_specs=[pl.BlockSpec(memory_space=pltpu.SMEM), vmem, last, last]
        + [vmem] * (2 + len(received)),
        out_specs=vmem,
        out_shape=jax.ShapeDtypeStruct((m, rows), BF16),
        compiler_params=params(24, 1),
        name="output",
    )(core, stream, own, swapped, near, hand, *received)


def on_device(
    residual,
    queries,
    new_keys,
    new_values,
    cache_keys,
    cache_values,
    cache_lengths,
    slot_of_row,
    out_weight,
    norm_gain,
    gate_weight,
    up_weight,
    down_weight,
):
    chips = Chips(lax.axis_size("sec"))
    core, chip = chips.core, chips.chip
    slots = slot_of_row.shape[0]
    local = slots // chips.devices
    m = residual.shape[0]
    wide = 2 * m

    mine, others = chips.distances(True), chips.distances(False)
    zero, one = jnp.zeros((1,), jnp.int32), jnp.ones((1,), jnp.int32)
    from_chips = chip ^ jnp.concatenate([zero, mine, others, one])
    swapped_core = jnp.concatenate([zero, 0 * mine, 0 * others + 1, zero])
    first = 2 * from_chips + (core ^ swapped_core)
    from_devices = jnp.stack([first, first ^ 1], axis=1).reshape(-1, 1)
    slot_ids = (from_devices * local + jnp.arange(local, dtype=jnp.int32)[None, :]).reshape(1, -1)
    pick = (slot_of_row[:, None] == slot_ids).astype(BF16)
    core_id = core.reshape(1)

    attended = attend(queries, new_keys, new_values, cache_keys, cache_values, cache_lengths)
    both = jnp.concatenate([attended, chips.swap(attended)])
    received = [chips.step(both, s) for s in chips.steps]
    near = chips.near(attended)
    swapped = [chips.swap(r) for r in received]
    pieces = [both] + received + swapped + [near, chips.swap(near)]
    stream = project(pick, out_weight, residual, pieces)

    other = chips.swap(stream)
    both = jnp.where(
        core == 0,
        jnp.concatenate([stream, other], axis=1),
        jnp.concatenate([other, stream], axis=1),
    )
    received = [chips.step(both, s) for s in chips.steps]
    near = chips.near(stream)
    swapped = [chips.swap(r) for r in received]
    pieces = [both] + received + swapped + [near, chips.swap(near)]
    gain = norm_gain.reshape(chips.count, 1, wide)
    hidden = hidden_units(
        jnp.concatenate([from_chips, core_id]), gain, pieces, gate_weight, up_weight
    )

    own = partial_sums(
        chip ^ jnp.concatenate([others, one, zero]), hidden, down_weight, wide
    )
    own_swapped = chips.swap(own)
    *sums, near_sum = chip_sums(
        jnp.concatenate([chip ^ mine, core_id]), hidden, down_weight, own, own_swapped
    )
    received = [chips.step(x, s) for x, s in zip(sums, chips.steps)]
    near = chips.near(near_sum)
    hand = chips.swap(handover(core_id, received))
    return output(core_id, stream, own, own_swapped, near, hand, received)


def solution(mesh):
    in_specs = (
        P("sec", "group"),
        P(("group", "sec"), None),
        P(("group", "sec"), None),
        P(("group", "sec"), None),
        P(("group", "sec"), None, None),
        P(("group", "sec"), None, None),
        P(("group", "sec")),
        P("group"),
        P("sec", None),
        P(),
        P("sec", None),
        P("sec", None),
        P("sec", None),
    )
    out_specs = P("sec", "group")
    return jax.shard_map(
        on_device, mesh=mesh, in_specs=in_specs, out_specs=out_specs, check_vma=False
    )
```

```python
import functools
import math

import jax
import jax.numpy as jnp
from jax import lax
from jax.experimental import pallas as pl
from jax.experimental.pallas import tpu as pltpu
from jax.sharding import PartitionSpec as P


H = 32
KVH = 4
HD = 128

EPSILON = 1e-05

F32 = jnp.float32
BF16 = jnp.bfloat16
NT = (((1,), (1,)), ((), ()))
MIB = 1 << 20


SMEM = pl.BlockSpec(memory_space=pltpu.SMEM)
VMEM = pl.BlockSpec(memory_space=pltpu.VMEM)
HBM = pl.BlockSpec(memory_space=pltpu.HBM)


def params(mib):
    return pltpu.CompilerParams(vmem_limit_bytes=int(mib * MIB))


def fetch(source, target, sems, first, parts):
    rows = source.shape[0] // parts
    copies = [
        pltpu.make_async_copy(
            source.at[pl.ds(i * rows, rows)], target.at[pl.ds(i * rows, rows)], sems.at[first + i]
        )
        for i in range(parts)
    ]
    for copy in copies:
        copy.start()
    return copies


def parts_of(rows):
    return 4 if rows % 64 == 0 else 1


class Chips:
    def __init__(self, devices):
        self.devices = devices
        self.count = devices // 2
        assert devices == 2 * self.count and self.count & (self.count - 1) == 0
        assert self.count > 2
        far = list(range(self.count - 1, 1, -1))
        self.steps = list(zip(far[0::2], far[1::2]))

    def swap(self, x):
        return lax.ppermute(x, "sec", [(i, i ^ 1) for i in range(self.devices)])

    def near(self, x):
        return lax.ppermute(x, "sec", [(i, i ^ 2) for i in range(self.devices)])

    def far(self, x, step):
        distances = self.steps[step]
        pairs = [(i, i ^ (2 * distances[i % 2])) for i in range(self.devices)]
        return lax.ppermute(x, "sec", pairs)

    def gather(self, both, mine):
        count = len(self.steps)
        received = [self.far(both, j) for j in range(count)]
        near = self.near(mine)
        swapped = [self.swap(r) for r in received]
        return [both] + received + swapped + [near, self.swap(near)]


def chip_ids(me, steps):
    core, chip = me % 2, me // 2
    mine = [chip ^ jnp.where(core == 0, a, b) for a, b in steps]
    others = [chip ^ jnp.where(core == 0, b, a) for a, b in steps]
    return [chip] + mine + others + [chip ^ 1]


def attention_kernel(
    me_ref, lens_ref, q_hbm, nk_hbm, nv_hbm, k_hbm, v_hbm, o_ref, q_ref, nk_ref, nv_ref, k_ref, v_ref, sems
):
    slots, positions = k_ref.shape[1], k_ref.shape[2]
    small = [
        pltpu.make_async_copy(a, b, sems.at[2 * KVH + i])
        for i, (a, b) in enumerate([(q_hbm, q_ref), (nk_hbm, nk_ref), (nv_hbm, nv_ref)])
    ]
    for copy in small:
        copy.start()
    large = []
    for k in range(KVH):
        for i, (a, b) in enumerate([(k_hbm, k_ref), (v_hbm, v_ref)]):
            copy = pltpu.make_async_copy(
                a.at[:, :, pl.ds(k * HD, HD)], b.at[k], sems.at[2 * k + i]
            )
            copy.start()
            large.append(copy)
    grouped = H // KVH
    rows = grouped * slots
    scaling = 1.0 / math.sqrt(HD)
    row_slot = lax.broadcasted_iota(jnp.int32, (rows, positions), 0) % slots
    position = lax.broadcasted_iota(jnp.int32, (rows, positions), 1)
    bias = jnp.concatenate(
        [
            jnp.where((row_slot == s) & (position < lens_ref[s]), 0.0, -jnp.inf)
            for s in range(slots)
        ],
        axis=1,
    )
    for copy in small:
        copy.wait()
    for k in range(KVH):
        at = slice(k * HD, (k + 1) * HD)
        heads = [slice((k * grouped + g) * HD, (k * grouped + g + 1) * HD) for g in range(grouped)]
        query = jnp.concatenate([q_ref[:, h].astype(F32) for h in heads], axis=0)
        large[2 * k].wait()
        keys = k_ref[k].reshape(slots * positions, HD)
        scores = lax.dot_general(query.astype(BF16), keys, NT, preferred_element_type=F32)
        scores = scores * scaling + bias
        new_key = jnp.concatenate([nk_ref[:, at].astype(F32)] * grouped, axis=0)
        fresh = jnp.sum(query * new_key, axis=1, keepdims=True) * scaling
        highest = jnp.maximum(jnp.max(scores, axis=1, keepdims=True), fresh)
        weights = jnp.exp(scores - highest)
        fresh_weight = jnp.exp(fresh - highest)
        inverse = 1.0 / (jnp.sum(weights, axis=1, keepdims=True) + fresh_weight)
        probs = (weights * inverse).astype(BF16)
        fresh_prob = (fresh_weight * inverse).astype(BF16).astype(F32)
        large[2 * k + 1].wait()
        values = v_ref[k].reshape(slots * positions, HD)
        mixture = jnp.dot(probs, values, preferred_element_type=F32)
        new_value = jnp.concatenate([nv_ref[:, at].astype(F32)] * grouped, axis=0)
        mixture = mixture + fresh_prob * new_value
        for g, h in enumerate(heads):
            o_ref[:, h] = mixture[g * slots : (g + 1) * slots].astype(BF16)


def attend(me, queries, new_keys, new_values, cache_keys, cache_values, cache_lengths):
    cache = pltpu.VMEM((KVH,) + cache_keys.shape[:2] + (HD,), BF16)
    return pl.pallas_call(
        attention_kernel,
        in_specs=[SMEM, SMEM] + [HBM] * 5,
        out_specs=VMEM,
        out_shape=jax.ShapeDtypeStruct(queries.shape, BF16),
        scratch_shapes=[
            pltpu.VMEM(queries.shape, BF16),
            pltpu.VMEM(new_keys.shape, BF16),
            pltpu.VMEM(new_values.shape, BF16),
            cache,
            cache,
            pltpu.SemaphoreType.DMA((2 * KVH + 3,)),
        ],
        compiler_params=params(56.5),
        name="attention",
    )(me, cache_lengths, queries, new_keys, new_values, cache_keys, cache_values)


def first_fetch_kernel(weight_hbm, residual_hbm, gain_ref, weight_ref, residual_ref, o_ref, sems):
    parts = parts_of(weight_hbm.shape[0])
    copies = fetch(weight_hbm, weight_ref, sems, 0, parts)
    copies += fetch(residual_hbm, residual_ref, sems, parts, 1)
    rows = o_ref.shape[1]

    @pl.loop(0, o_ref.shape[0], step=128)
    def _(c):
        at = pl.ds(pl.multiple_of(c, 128), 128)
        o_ref[at, :] = jnp.broadcast_to(gain_ref[:, at], (rows, 128)).T

    for copy in copies:
        copy.wait()


def first_fetch(out_weight, residual, norm_gain):
    width = norm_gain.shape[0]
    return pl.pallas_call(
        first_fetch_kernel,
        in_specs=[HBM, HBM, VMEM],
        out_specs=[VMEM] * 3,
        out_shape=[
            jax.ShapeDtypeStruct(out_weight.shape, BF16),
            jax.ShapeDtypeStruct(residual.shape, BF16),
            jax.ShapeDtypeStruct((width, residual.shape[1]), F32),
        ],
        scratch_shapes=[pltpu.SemaphoreType.DMA((parts_of(out_weight.shape[0]) + 1,))],
        compiler_params=params(40),
        name="fetch1",
    )(out_weight, residual, norm_gain.reshape(1, width))


def second_fetch_kernel(source, *refs):
    targets, sems = refs[:-1], refs[-1]
    rows = targets[0].shape[0]
    copies = [
        pltpu.make_async_copy(source.at[pl.ds(i * rows, rows)], target, sems.at[i])
        for i, target in enumerate(targets)
    ]
    for copy in copies:
        copy.start()
    for copy in copies:
        copy.wait()


def second_fetch(weight, tile, parts):
    return pl.pallas_call(
        second_fetch_kernel,
        in_specs=[HBM],
        out_specs=[VMEM] * parts,
        out_shape=[jax.ShapeDtypeStruct((tile, weight.shape[1]), BF16)] * parts,
        scratch_shapes=[pltpu.SemaphoreType.DMA((parts,))],
        compiler_params=params(42),
        name="fetch2",
    )(weight)


def pair_kernel(me_ref, mine_ref, other_ref, o_ref):
    place_halves(me_ref[0] % 2 == 0, mine_ref[...], other_ref[...], o_ref)


def place_halves(first, mine, other, o_ref):
    m = mine.shape[0]
    o_ref[:m, :] = jnp.where(first, mine, other)
    o_ref[m:, :] = jnp.where(first, other, mine)


def pair(me, mine, other):
    m, rows = mine.shape
    return pl.pallas_call(
        pair_kernel,
        in_specs=[SMEM, VMEM, VMEM],
        out_specs=VMEM,
        out_shape=jax.ShapeDtypeStruct((2 * m, rows), BF16),
        compiler_params=params(4),
        name="pair",
    )(me, mine, other)


def projection_kernel(steps, me_ref, rows_ref, weight_ref, residual_ref, *refs):
    pieces = 2 * len(steps) + 3
    piece_refs, o_ref, slots_ref = refs[:pieces], refs[pieces], refs[pieces + 1]
    local = piece_refs[-1].shape[0]
    for i, ref in enumerate(piece_refs[:-2]):
        slots_ref[2 * local * i : 2 * local * (i + 1), :] = ref[...]
    near = jnp.concatenate([ref[...].astype(F32) for ref in piece_refs[-2:]])
    slots_ref[2 * local * (pieces - 2) :, :] = near.astype(BF16)

    me = me_ref[0]
    chips = chip_ids(me, steps)
    slots, rows = slots_ref.shape[0], rows_ref.shape[1]
    at = lax.broadcasted_iota(jnp.int32, (slots, rows), 0)
    held = at % local
    for i, chip in enumerate(chips):
        core = (me + (1 if len(steps) < i <= 2 * len(steps) else 0)) % 2
        for j, device in enumerate([2 * chip + core, 2 * chip + 1 - core]):
            held += jnp.where(at // local == 2 * i + j, device * local, 0)
    pick = jnp.where(held == rows_ref[...], 1.0, 0.0).T.astype(BF16)

    width = weight_ref.shape[1]
    part = min(width, 1024)
    total = residual_ref[...].astype(F32)
    for c in range(0, width, part):
        ordered = jnp.dot(pick, slots_ref[:, c : c + part], preferred_element_type=F32)
        total += lax.dot_general(
            weight_ref[:, c : c + part], ordered.astype(BF16), NT, preferred_element_type=F32
        )
    o_ref[...] = total.astype(BF16)


def project(steps, me, slot_of_row, out_weight, residual, pieces):
    m, rows = residual.shape
    return pl.pallas_call(
        functools.partial(projection_kernel, steps),
        in_specs=[SMEM] + [VMEM] * (3 + len(pieces)),
        out_specs=VMEM,
        out_shape=jax.ShapeDtypeStruct((m, rows), BF16),
        scratch_shapes=[pltpu.VMEM((rows, out_weight.shape[1]), BF16)],
        compiler_params=params(12),
        name="projection",
    )(me, slot_of_row.reshape(1, rows), out_weight, residual, *pieces)


def hidden_kernel(steps, tile, me_ref, gain_ref, gate_hbm, up_hbm, down_hbm, *refs):
    pieces = 2 * len(steps) + 3
    piece_refs, up_refs = refs[:pieces], refs[pieces:-7]
    o_ref, down_ref, gate_ref, rest_ref, x_ref, near_ref, sems = refs[-7:]
    parts = gate_hbm.shape[0] // tile
    held = len(up_refs)
    gate_copies, up_copies = [], []
    for i in range(parts):
        rows = pl.ds(i * tile, tile)
        copy = pltpu.make_async_copy(gate_hbm.at[rows], gate_ref.at[rows], sems.at[i])
        copy.start()
        gate_copies.append(copy)
        if i >= held:
            copy = pltpu.make_async_copy(
                up_hbm.at[rows], rest_ref.at[pl.ds((i - held) * tile, tile)], sems.at[parts + i]
            )
            copy.start()
            up_copies.append(copy)
    copies = fetch(down_hbm, down_ref, sems, 2 * parts, parts_of(down_hbm.shape[0]))
    wide = piece_refs[0].shape[0]
    me = me_ref[0]
    place_halves(me % 2 == 0, piece_refs[-2][...], piece_refs[-1][...], near_ref)
    squares = None
    for chip, ref in zip(chip_ids(me, steps), list(piece_refs[:-2]) + [near_ref]):
        at = pl.ds(pl.multiple_of(chip * wide, 128), wide)
        value = ref[...].astype(F32)
        x_ref[at, :] = (value * gain_ref[at, :]).astype(BF16)
        square = value * value
        squares = square if squares is None else squares + square
    mean = jnp.sum(squares, axis=0, keepdims=True) * (1.0 / x_ref.shape[0])
    scale = lax.rsqrt(mean + EPSILON)
    for i in range(parts):
        at = slice(i * tile, (i + 1) * tile)
        if i < held:
            weights = up_refs[i][...]
        else:
            up_copies[i - held].wait()
            weights = rest_ref[(i - held) * tile : (i - held + 1) * tile, :]
        up = jnp.dot(weights, x_ref[...], preferred_element_type=F32) * scale
        gate_copies[i].wait()
        gate = jnp.dot(gate_ref[at, :], x_ref[...], preferred_element_type=F32) * scale
        units = gate / (1.0 + jnp.exp(-gate)) * up
        o_ref[:, at] = units.T.astype(BF16)
    for copy in copies:
        copy.wait()


def unit_tile(units):
    return 256 if units % 256 == 0 else units


def hidden_units(steps, me, gain, gate_weight, up_weight, up_held, down_weight, pieces):
    units, width = gate_weight.shape
    wide, rows = pieces[0].shape
    tile = unit_tile(units)
    return pl.pallas_call(
        functools.partial(hidden_kernel, steps, tile),
        in_specs=[SMEM, VMEM, HBM, HBM, HBM] + [VMEM] * (len(pieces) + len(up_held)),
        out_specs=[VMEM, VMEM],
        out_shape=[
            jax.ShapeDtypeStruct((rows, units), BF16),
            jax.ShapeDtypeStruct(down_weight.shape, BF16),
        ],
        scratch_shapes=[
            pltpu.VMEM(gate_weight.shape, BF16),
            pltpu.VMEM((max(units - len(up_held) * tile, 16), width), BF16),
            pltpu.VMEM((width, rows), BF16),
            pltpu.VMEM((wide, rows), BF16),
            pltpu.SemaphoreType.DMA((2 * (units // tile) + parts_of(units),)),
        ],
        compiler_params=params(25),
        name="hidden",
    )(me, gain, gate_weight, up_weight, down_weight, *pieces, *up_held)


def down_block(hidden_ref, weight_ref, chip, wide):
    at = pl.ds(pl.multiple_of(chip * wide, 128), wide)
    return jnp.dot(hidden_ref[...], weight_ref[:, at], preferred_element_type=F32)


def theirs_kernel(steps, me_ref, hidden_ref, weight_ref, o_ref):
    chips = chip_ids(me_ref[0], steps)
    count = len(steps)
    for j, chip in enumerate(chips[count + 1 :] + chips[:1]):
        o_ref[j] = down_block(hidden_ref, weight_ref, chip, o_ref.shape[2]).astype(BF16)


def partial_sums(steps, me, hidden, down_weight, wide):
    return pl.pallas_call(
        functools.partial(theirs_kernel, steps),
        in_specs=[SMEM, VMEM, VMEM],
        out_specs=VMEM,
        out_shape=jax.ShapeDtypeStruct((len(steps) + 2, hidden.shape[0], wide), BF16),
        compiler_params=params(12),
        name="theirs",
    )(me, hidden, down_weight)


def mine_kernel(steps, me_ref, hidden_ref, weight_ref, own_ref, swapped_ref, *o_refs):
    me = me_ref[0]
    chips = chip_ids(me, steps)
    count = len(steps)
    for j in range(count):
        total = down_block(hidden_ref, weight_ref, chips[1 + j], o_refs[j].shape[1])
        o_refs[j][...] = (total + swapped_ref[j].astype(F32)).astype(BF16)
    near = own_ref[count].astype(F32) + swapped_ref[count].astype(F32)
    o_refs[count][...] = half_of(me % 2, near).astype(BF16)


def chip_sums(steps, me, hidden, down_weight, own, swapped):
    rows, wide = own.shape[1:]
    return pl.pallas_call(
        functools.partial(mine_kernel, steps),
        in_specs=[SMEM] + [VMEM] * 4,
        out_specs=[VMEM] * (len(steps) + 1),
        out_shape=[jax.ShapeDtypeStruct((rows, wide), BF16)] * len(steps)
        + [jax.ShapeDtypeStruct((rows, wide // 2), BF16)],
        compiler_params=params(12),
        name="mine",
    )(me, hidden, down_weight, own, swapped)


def half_of(core, value):
    m = value.shape[1] // 2
    return jnp.where(core == 0, value[:, :m], value[:, m:])


def received_sum(refs):
    total = refs[0][...].astype(F32)
    for ref in refs[1:]:
        total += ref[...].astype(F32)
    return total


def handover_kernel(me_ref, *refs):
    refs[-1][...] = half_of(1 - me_ref[0] % 2, received_sum(refs[:-1])).astype(BF16)


def handover(me, received):
    rows, wide = received[0].shape
    return pl.pallas_call(
        handover_kernel,
        in_specs=[SMEM] + [VMEM] * len(received),
        out_specs=VMEM,
        out_shape=jax.ShapeDtypeStruct((rows, wide // 2), BF16),
        compiler_params=params(12),
        name="handover",
    )(me, *received)


def output_kernel(me_ref, stream_ref, own_ref, owns_ref, near_ref, hand_ref, *refs):
    last = own_ref.shape[0] - 1
    total = received_sum(refs[:-1])
    total += own_ref[last].astype(F32) + owns_ref[last].astype(F32)
    total = half_of(me_ref[0] % 2, total) + near_ref[...].astype(F32) + hand_ref[...].astype(F32)
    refs[-1][...] = (stream_ref[...].astype(F32) + total.T).astype(BF16)


def output(me, stream, own, swapped, near, hand, received):
    m, rows = stream.shape
    return pl.pallas_call(
        output_kernel,
        in_specs=[SMEM] + [VMEM] * (5 + len(received)),
        out_specs=VMEM,
        out_shape=jax.ShapeDtypeStruct((m, rows), BF16),
        compiler_params=params(12),
        name="output",
    )(me, stream, own, swapped, near, hand, *received)


def on_device(
    residual,
    queries,
    new_keys,
    new_values,
    cache_keys,
    cache_values,
    cache_lengths,
    slot_of_row,
    out_weight,
    norm_gain,
    gate_weight,
    up_weight,
    down_weight,
):
    chips = Chips(lax.axis_size("sec"))
    steps = chips.steps
    me = lax.axis_index("sec").reshape(1)
    wide = 2 * residual.shape[0]

    attended = attend(me, queries, new_keys, new_values, cache_keys, cache_values, cache_lengths)
    both = jnp.concatenate([attended, chips.swap(attended)])
    out_weight, residual, gain = first_fetch(out_weight, residual, norm_gain)
    pieces = chips.gather(both, attended)
    stream = project(steps, me, slot_of_row, out_weight, residual, pieces)

    other = chips.swap(stream)
    both = pair(me, stream, other)
    tile = unit_tile(up_weight.shape[0])
    up_held = second_fetch(up_weight, tile, (up_weight.shape[0] // tile + 1) // 2)
    pieces = chips.gather(both, stream)
    hidden, down_weight = hidden_units(
        steps, me, gain, gate_weight, up_weight, up_held, down_weight, pieces
    )

    own = partial_sums(steps, me, hidden, down_weight, wide)
    own_swapped = chips.swap(own)
    *sums, near_sum = chip_sums(steps, me, hidden, down_weight, own, own_swapped)
    received = [chips.far(x, j) for j, x in enumerate(sums)]
    near = chips.near(near_sum)
    hand = chips.swap(handover(me, received))
    return output(me, stream, own, own_swapped, near, hand, received)


def solution(mesh):
    in_specs = (
        P("sec", "group"),
        P(("group", "sec"), None),
        P(("group", "sec"), None),
        P(("group", "sec"), None),
        P(("group", "sec"), None, None),
        P(("group", "sec"), None, None),
        P(("group", "sec")),
        P("group"),
        P("sec", None),
        P(),
        P("sec", None),
        P("sec", None),
        P("sec", None),
    )
    out_specs = P("sec", "group")

    return jax.shard_map(
        on_device, mesh=mesh, in_specs=in_specs, out_specs=out_specs, check_vma=False
    )
```
